32 devices in a mesh: view: 4 (over z), tile: 8 (over y, x, core).
Axes of the slice: x: 2, y: 2, z: 4, core: 2. Of those that a mesh axis runs over, the one named last changes fastest.
Arguments:
- sdf_value: float32 [6144, 256], P(('view', 'tile')), may hold values from -1 to 1
- weight: float32 [6144, 256], P(('view', 'tile')), may hold values from 0.25 to 4
- color: float32 [3, 6144, 256], P(None, ('view', 'tile')), may hold values from 0 to 1
- voxel_index: int32 [6144, 256], P(('view', 'tile')), may hold values from 0 to 511
- valid: int32 [6144, 256], P(('view', 'tile')), may hold values 0 or 1
- list_count: int32 [6144], P(('view', 'tile')), may hold values from 1 to 256
- list_key: int32 [6144], P(('view', 'tile')), may hold values from 0 to 2047, as said below
- owner_slot: int32 [2048], replicated, may hold values from 0 to 2047, as said below
Outputs:
- joined_tsdf: float32 [2048, 512], P(('view', 'tile'))
- joined_color: float32 [2048, 3, 512], P(('view', 'tile'))
- block_counts: int32 [2048], replicated
The draws below stay inside these ranges and needn't reach their ends.
Inputs may be any that keep to these rules, and one draw needn't show every extreme that they name: `owner_slot`: each block key has one storage row and each row one key. Of the 192 lists of one device, at most 24 have a storage row owner_slot[list_key] among the 64 rows of any one device; some device receives exactly 24 lists from every device.
All inputs are finite; a program needn't handle non-finite values. No bound on the sum of `valid` on one device may be relied on, other than what follows from the above.
Results may differ from the reference program's by a relative error of at most 0.0037.
Values may be sent and summed in bfloat16 or wider, within the bound.
A program may use at most 64 MiB of HBM per device.

```python
import math
import jax
import jax.numpy as jnp
from jax import lax

VOX = 512
PTS = 256
LISTS_DEV = 192
BLK_DEV = 64
CAP = 24
LISTS = 6144
NBLK = 2048
DEVICES = 32


def routing(key):
    base = jax.random.fold_in(key, 7)
    slot_of = jax.random.permutation(jax.random.fold_in(base, 1), NBLK).astype(jnp.int32)
    key_of = jnp.zeros((NBLK,), jnp.int32).at[slot_of].set(jnp.arange(NBLK, dtype=jnp.int32))
    hottest = jax.random.randint(jax.random.fold_in(base, 2), (), 0, DEVICES).astype(jnp.int32)

    def one_source(sub):
        picks = jax.random.permutation(jax.random.fold_in(sub, 0), (DEVICES - 1) * CAP)[:LISTS_DEV - CAP].astype(jnp.int32)
        others = picks // CAP
        others = jnp.where(others >= hottest, others + 1, others)
        targets = jnp.concatenate([jnp.full((CAP,), hottest, jnp.int32), others])
        targets = jax.random.permutation(jax.random.fold_in(sub, 1), targets)
        local_rows = jax.random.randint(jax.random.fold_in(sub, 2), (LISTS_DEV,), 0, BLK_DEV).astype(jnp.int32)
        return key_of[targets * BLK_DEV + local_rows]
    random_subkeys = jax.random.split(jax.random.fold_in(base, 3), DEVICES)
    list_keys = jax.vmap(one_source)(random_subkeys).reshape(-1).astype(jnp.int32)
    return (slot_of, list_keys)


def draw_owner_slot(key, part):
    return routing(key)[0]


def draw_list_key(key, part):
    return routing(key)[1]


def place_ends(array, stream_key, least, top_value):
    longest = array.shape.index(max(array.shape))
    spots = []
    for shift in (0, 1):
        where = [jax.random.randint(jax.random.fold_in(stream_key, axis), (), 0, length) for axis, length in enumerate(array.shape)]
        where[longest] = (where[longest] + shift) % array.shape[longest]
        spots.append(tuple(where))
    return array.at[spots[0]].set(least).at[spots[1]].set(top_value)


def levels(key, shape, cuts, low, largest):
    gain = 1.0
    for dim, shards_of in cuts:
        steps = jax.random.uniform(jax.random.fold_in(jax.random.fold_in(key, 6), dim), (shards_of,), jnp.float32, low / len(cuts), largest / len(cuts))
        gain = gain * jnp.repeat(jnp.exp(steps), shape[dim] // shards_of).reshape((-1,) + (1,) * (len(shape) - 1 - dim))
    return gain


def setup_inputs(seed: int = 0) -> dict:
    streams_of = jax.random.split(jax.random.key(seed), 9)
    sdf_value = jnp.clip(jax.random.uniform(streams_of[0], (LISTS, PTS), jnp.float32, -1.0, 1.0) * levels(streams_of[0], (LISTS, PTS), ((0, 32),), -0.4, 0.0), -1.0, 1.0)
    weight = jnp.clip(jnp.exp(math.log(4.0) - 2.7725887 * jax.random.uniform(streams_of[1], (LISTS, PTS), jnp.float32) ** levels(streams_of[1], (LISTS, PTS), ((0, 32),), -0.2, 0.2)), 0.25, 4.0)
    color = jnp.clip(1.0 * jax.random.uniform(streams_of[2], (3, LISTS, PTS), jnp.float32) ** levels(streams_of[2], (3, LISTS, PTS), ((1, 32),), -0.2, 0.2), 0.0, 1.0)
    voxel_index = place_ends(jax.random.randint(streams_of[3], (LISTS, PTS), 0, VOX), jax.random.fold_in(streams_of[3], 1), 0, VOX - 1).astype(jnp.int32)
    valid = place_ends((jax.random.randint(streams_of[4], (LISTS, PTS), 0, 8) < 7).astype(jnp.int32), jax.random.fold_in(streams_of[4], 1), 0, 1)
    list_count = place_ends(jax.random.randint(streams_of[5], (LISTS,), 1, PTS + 1), jax.random.fold_in(streams_of[5], 1), 1, PTS).astype(jnp.int32)
    list_key = draw_list_key(jax.random.fold_in(streams_of[8], 71), 0)
    owner_slot = draw_owner_slot(jax.random.fold_in(streams_of[8], 71), 0)
    return dict(sdf_value=sdf_value, weight=weight, color=color, voxel_index=voxel_index, valid=valid, list_count=list_count, list_key=list_key, owner_slot=owner_slot)


def reference(sdf_value, weight, color, voxel_index, valid, list_count, list_key, owner_slot):
    points = sdf_value.shape[1]
    position = jnp.arange(points, dtype=jnp.int32)
    live_mask = ((position[None, :] < list_count[:, None]) & (valid == 1)).astype(jnp.float32)
    scaled = live_mask * weight
    channels = jnp.stack([live_mask, scaled, scaled * sdf_value, scaled * color[0], scaled * color[1], scaled * color[2]], axis=-1)
    rounded = lax.optimization_barrier(channels.astype(jnp.bfloat16))
    value_entries = rounded.astype(jnp.float32)
    storage = owner_slot[list_key].astype(jnp.int32)
    segment_ids = (storage[:, None] * VOX + voxel_index).astype(jnp.int32)
    voxel_sums = jax.ops.segment_sum(value_entries.reshape(-1, 6), segment_ids.reshape(-1), num_segments=NBLK * VOX)
    voxel_sums = voxel_sums.reshape(NBLK, VOX, 6)
    block_counts = jnp.sum(voxel_sums[:, :, 0], axis=1).astype(jnp.int32)
    divisor = jnp.maximum(voxel_sums[:, :, 1], 1.0)
    joined_tsdf = voxel_sums[:, :, 2] / divisor
    joined_color = jnp.transpose(voxel_sums[:, :, 3:6] / divisor[:, :, None], (0, 2, 1))
    return joined_tsdf, joined_color, block_counts
```

```python
import functools

import jax
import jax.numpy as jnp
from jax import lax
from jax.experimental import pallas as pl
from jax.experimental.pallas import tpu as pltpu
from jax.sharding import PartitionSpec as P

VOX = 512
HI = 8
LO = VOX // HI
CH = 5
AXES = ("view", "tile")
NT = (((1,), (1,)), ((), ()))


def pack_kernel(n, cap, slot_ref, live_count_ref, sdf_ref, weight_ref, color_ref, voxel_ref, valid_ref, out_ref):
    lists, points = sdf_ref.shape
    position = lax.broadcasted_iota(jnp.int32, (lists, points), 1)
    live = (position < live_count_ref[...]) & (valid_ref[...] == 1)
    scaled = jnp.where(live, weight_ref[...], 0.0)
    slots = lax.broadcasted_iota(jnp.int32, (n * cap, lists), 0)
    placement = jnp.where(slots == slot_ref[...], 1.0, 0.0).astype(jnp.bfloat16)
    for c in range(CH + 1):
        if c == 0:
            value = scaled
        elif c == 1:
            value = scaled * sdf_ref[...]
        elif c < CH:
            value = scaled * color_ref[c - 2]
        else:
            value = (voxel_ref[...] - VOX // 2).astype(jnp.float32)
        placed = jnp.dot(
            placement, value.astype(jnp.bfloat16), preferred_element_type=jnp.float32
        ).astype(jnp.bfloat16)
        for d in range(n):
            out_ref[d, c * cap : (c + 1) * cap, :] = placed[d * cap : (d + 1) * cap, :]


def join_kernel(
    n, tiles, cap, group, q, send_ref, meta_ref, tsdf_ref, color_ref, counts_ref,
    got, got_meta, block, parts, acc, hist, send_sem, recv_sem, meta_send_sem, meta_recv_sem,
):
    me = lax.axis_index("view") * tiles + lax.axis_index("tile")
    points = send_ref.shape[-1]
    blocks_dev = tsdf_ref.shape[0]
    rows = CH * HI

    def mesh_id(d):
        return (d // tiles, d % tiles)

    barrier = pltpu.get_barrier_semaphore()

    @pl.loop(1, n)
    def _(i):
        pl.semaphore_signal(
            barrier, inc=1, device_id=mesh_id(lax.rem(me + i, n)),
            device_id_type=pl.DeviceIdType.MESH,
        )

    own = pltpu.make_async_copy(send_ref.at[me], got.at[0], recv_sem.at[0])
    own_meta = pltpu.make_async_copy(meta_ref.at[me], got_meta.at[0], meta_recv_sem.at[0])
    own.start()
    own_meta.start()
    acc[...] = jnp.zeros_like(acc)
    hist[...] = jnp.zeros_like(hist)
    pl.semaphore_wait(barrier, n - 1)

    def copies(i):
        d = lax.rem(me + i, n)
        return (
            pltpu.make_async_remote_copy(
                src_ref=meta_ref.at[d], dst_ref=got_meta.at[i],
                send_sem=meta_send_sem.at[i], recv_sem=meta_recv_sem.at[i],
                device_id=mesh_id(d), device_id_type=pl.DeviceIdType.MESH,
            ),
            pltpu.make_async_remote_copy(
                src_ref=send_ref.at[d], dst_ref=got.at[i],
                send_sem=send_sem.at[i], recv_sem=recv_sem.at[i],
                device_id=mesh_id(d), device_id_type=pl.DeviceIdType.MESH,
            ),
        )

    @pl.loop(1, n)
    def _(i):
        for copy in copies(i):
            copy.start()

    hi_ids = lax.broadcasted_iota(jnp.int32, (HI, points), 0).astype(jnp.float32)
    lo_ids = lax.broadcasted_iota(jnp.int32, (LO, points), 0).astype(jnp.float32)
    lanes = q * 128
    hist_hi = lax.broadcasted_iota(jnp.int32, (hist.shape[0], lanes), 0).astype(jnp.float32)
    hist_lo = lax.broadcasted_iota(jnp.int32, (128, lanes), 0).astype(jnp.float32)
    row_ids = lax.broadcasted_iota(jnp.int32, (blocks_dev, group * cap), 0).astype(jnp.float32)

    def one_source(i, j):
        pltpu.make_async_copy(got_meta.at[i], got_meta.at[i], meta_recv_sem.at[i]).wait()
        pltpu.make_async_copy(got.at[i], got.at[i], recv_sem.at[i]).wait()
        block[...] = got[i].astype(jnp.float32)
        voxel = block[CH * cap : (CH + 1) * cap, :] + float(VOX // 2)
        high = jnp.floor(voxel * (1.0 / LO))
        low = voxel - high * float(LO)
        for s in range(cap):
            mask = jnp.broadcast_to(high[s : s + 1, :], (HI, points)) == hi_ids
            a = jnp.concatenate(
                [
                    jnp.where(
                        mask,
                        jnp.broadcast_to(block[c * cap + s : c * cap + s + 1, :], (HI, points)),
                        0.0,
                    )
                    for c in range(CH)
                ],
                axis=0,
            ).astype(jnp.bfloat16)
            b = jnp.where(
                jnp.broadcast_to(low[s : s + 1, :], (LO, points)) == lo_ids, 1.0, 0.0
            ).astype(jnp.bfloat16)
            parts[j * cap + s] = lax.dot_general(a, b, NT, preferred_element_type=jnp.float32)
        meta = got_meta[i]
        storage = jnp.concatenate([meta[1 + k : 2 + k, :] for k in range(q)], axis=1)
        counts = jnp.concatenate([meta[1 + q + k : 2 + q + k, :] for k in range(q)], axis=1)
        s_hi = jnp.floor(storage * (1.0 / 128))
        s_lo = storage - s_hi * 128.0
        a = jnp.where(s_hi == hist_hi, counts, 0.0).astype(jnp.bfloat16)
        b = jnp.where(s_lo == hist_lo, 1.0, 0.0).astype(jnp.bfloat16)
        hist[...] += lax.dot_general(a, b, NT, preferred_element_type=jnp.float32)

    @pl.loop(0, n // group)
    def _(g):
        @pl.loop(0, group)
        def _(j):
            one_source(g * group + j, j)

        row = jnp.concatenate(
            [got_meta[g * group + j][0:1, 0:cap] for j in range(group)], axis=1
        )
        hot = jnp.where(row == row_ids, 1.0, 0.0).astype(jnp.bfloat16)
        for r in range(rows):
            acc[r] += jnp.dot(
                hot, parts[:, r, :].astype(jnp.bfloat16), preferred_element_type=jnp.float32
            )

    for h in range(HI):
        divisor = jnp.maximum(acc[h], 1.0)
        tsdf_ref[:, h * LO : (h + 1) * LO] = acc[HI + h] / divisor
        for k in range(3):
            color_ref[k, :, h * LO : (h + 1) * LO] = acc[(2 + k) * HI + h] / divisor
    counts_ref[...] = hist[...].astype(jnp.int32)

    @pl.loop(1, n)
    def _(i):
        for copy in copies(i):
            copy.wait_send()


def on_device(tiles, sdf_value, weight, color, voxel_index, valid, list_count, list_key, owner_slot):
    lists, points = sdf_value.shape
    n = lax.axis_size(AXES)
    blocks_all = owner_slot.shape[0]
    blocks_dev = blocks_all // n
    cap = 4 * lists // n
    q = -(-lists // 128)
    group = 1
    while 2 * group * cap <= 256 and n % (2 * group) == 0:
        group *= 2

    position = jnp.arange(points, dtype=jnp.int32)
    live_points = jnp.sum(
        ((position[None, :] < list_count[:, None]) & (valid == 1)).astype(jnp.int32), axis=1
    )
    key_match = list_key[:, None] == jnp.arange(blocks_all, dtype=jnp.int32)[None, :]
    storage = jnp.sum(jnp.where(key_match, owner_slot[None, :], 0), axis=1)
    owner = storage // blocks_dev
    row = storage % blocks_dev
    ids = jnp.arange(lists, dtype=jnp.int32)
    arrival = jnp.sum(
        ((owner[:, None] == owner[None, :]) & (ids[None, :] < ids[:, None])).astype(jnp.int32), axis=1
    )
    slot = owner * cap + arrival
    slot_row = (
        jnp.max(
            jnp.where(
                slot[None, :] == jnp.arange(n * cap, dtype=jnp.int32)[:, None], row[None, :], -1
            ),
            axis=1,
        )
        .astype(jnp.float32)
        .reshape(n, 1, cap)
    )
    slot_row = jnp.pad(slot_row, ((0, 0), (0, 0), (0, 128 - cap)), constant_values=-1.0)

    def lane_rows(x):
        x = jnp.pad(x.astype(jnp.float32), (0, q * 128 - lists)).reshape(1, q, 128)
        return jnp.broadcast_to(x, (n, q, 128))

    meta_rows = -(-(1 + 2 * q) // 8) * 8
    meta = jnp.concatenate(
        [
            slot_row,
            lane_rows(storage),
            lane_rows(live_points),
            jnp.zeros((n, meta_rows - 1 - 2 * q, 128), jnp.float32),
        ],
        axis=1,
    )
    send = pl.pallas_call(
        functools.partial(pack_kernel, n, cap),
        out_shape=jax.ShapeDtypeStruct((n, (CH + 1) * cap, points), jnp.bfloat16),
        in_specs=[pl.BlockSpec(memory_space=pltpu.VMEM)] * 7,
        out_specs=pl.BlockSpec(memory_space=pltpu.VMEM),
    )(slot[None, :], list_count[:, None], sdf_value, weight, color, voxel_index, valid)

    rows = CH * HI
    tsdf, joined, counts = pl.pallas_call(
        functools.partial(join_kernel, n, tiles, cap, group, q),
        out_shape=(
            jax.ShapeDtypeStruct((blocks_dev, VOX), jnp.float32),
            jax.ShapeDtypeStruct((3, blocks_dev, VOX), jnp.float32),
            jax.ShapeDtypeStruct((blocks_all // 128, 128), jnp.int32),
        ),
        in_specs=[pl.BlockSpec(memory_space=pl.ANY)] * 2,
        out_specs=(pl.BlockSpec(memory_space=pltpu.VMEM),) * 3,
        scratch_shapes=[
            pltpu.VMEM((n, (CH + 1) * cap, points), jnp.bfloat16),
            pltpu.VMEM((n, meta_rows, 128), jnp.float32),
            pltpu.VMEM(((CH + 1) * cap, points), jnp.float32),
            pltpu.VMEM((group * cap, rows, LO), jnp.float32),
            pltpu.VMEM((rows, blocks_dev, LO), jnp.float32),
            pltpu.VMEM((blocks_all // 128, 128), jnp.float32),
            pltpu.SemaphoreType.DMA((n,)),
            pltpu.SemaphoreType.DMA((n,)),
            pltpu.SemaphoreType.DMA((n,)),
            pltpu.SemaphoreType.DMA((n,)),
        ],
        compiler_params=pltpu.CompilerParams(collective_id=0, has_side_effects=True),
    )(send, meta)
    return tsdf, jnp.swapaxes(joined, 0, 1), counts.reshape(blocks_all)


def solution(mesh):
    return jax.shard_map(
        functools.partial(on_device, mesh.shape["tile"]),
        mesh=mesh,
        in_specs=(
            P(AXES, None),
            P(AXES, None),
            P(None, AXES, None),
            P(AXES, None),
            P(AXES, None),
            P(AXES),
            P(AXES),
            P(),
        ),
        out_specs=(P(AXES, None), P(AXES, None, None), P()),
        check_vma=False,
    )
```

```python
import functools

import jax
import jax.numpy as jnp
from jax import lax
from jax.experimental import pallas as pl
from jax.experimental.pallas import tpu as pltpu
from jax.sharding import PartitionSpec as P

VOX = 512
HI = 8
LO = VOX // HI
CH = 5
AXES = ("view", "tile")
NT = (((1,), (1,)), ((), ()))


def pack_kernel(n, cap, slot_ref, live_count_ref, sdf_ref, weight_ref, color_ref, voxel_ref, valid_ref, out_ref):
    lists, points = sdf_ref.shape
    position = lax.broadcasted_iota(jnp.int32, (lists, points), 1)
    live = (position < live_count_ref[...]) & (valid_ref[...] == 1)
    scaled = jnp.where(live, weight_ref[...], 0.0)
    slots = lax.broadcasted_iota(jnp.int32, (n * cap, lists), 0)
    placement = jnp.where(slots == slot_ref[...], 1.0, 0.0).astype(jnp.bfloat16)
    for c in range(CH + 1):
        if c == 0:
            value = scaled
        elif c == 1:
            value = scaled * sdf_ref[...]
        elif c < CH:
            value = scaled * color_ref[c - 2]
        else:
            value = (voxel_ref[...] - VOX // 2).astype(jnp.float32)
        placed = jnp.dot(
            placement, value.astype(jnp.bfloat16), preferred_element_type=jnp.float32
        ).astype(jnp.bfloat16)
        for d in range(n):
            out_ref[d, c * cap : (c + 1) * cap, :] = placed[d * cap : (d + 1) * cap, :]


def join_kernel(
    views, tiles, cap, q, send_ref, meta_ref, tsdf_ref, color_ref, counts_ref,
    got, got_meta, block, parts, acc, dense_send, dense_got, hist, hist_got,
    send_sem, recv_sem, meta_send_sem, meta_recv_sem,
    dense_send_sem, dense_recv_sem, hist_send_sem, hist_recv_sem,
):
    view = lax.axis_index("view")
    tile = lax.axis_index("tile")
    points = send_ref.shape[-1]
    blocks_dev = tsdf_ref.shape[0]
    rows = CH * HI
    slots = tiles * cap
    half = HI // 2

    def view_of(k):
        step = views - 1 - k
        if views & (views - 1):
            return lax.rem(view + step, views)
        partner = 0
        bit = 1
        while bit < views:
            mine = (view // bit) % 2
            flip = (step // bit) % 2
            partner = partner + bit * (mine + flip - 2 * mine * flip)
            bit *= 2
        return partner

    def tile_of(i):
        return lax.rem(tile + i, tiles)

    barrier = pltpu.get_barrier_semaphore()

    @pl.loop(1, tiles)
    def _(i):
        pl.semaphore_signal(
            barrier, inc=1, device_id=(view, tile_of(i)), device_id_type=pl.DeviceIdType.MESH
        )

    @pl.loop(0, views - 1)
    def _(k):
        pl.semaphore_signal(
            barrier, inc=1, device_id=(view_of(k), tile), device_id_type=pl.DeviceIdType.MESH
        )

    def own_copy(k):
        return pltpu.make_async_copy(
            send_ref.at[view_of(k) * tiles + tile], got.at[k * tiles], recv_sem.at[k * tiles]
        )

    own_meta = pltpu.make_async_copy(meta_ref.at[tile], got_meta.at[0], meta_recv_sem.at[0])
    own_meta.start()

    @pl.loop(0, views)
    def _(k):
        own_copy(k).start()

    hist[...] = jnp.zeros_like(hist)
    pl.semaphore_wait(barrier, tiles - 1 + views - 1)

    def meta_copy(i):
        return pltpu.make_async_remote_copy(
            src_ref=meta_ref.at[tile_of(i)], dst_ref=got_meta.at[i],
            send_sem=meta_send_sem.at[i], recv_sem=meta_recv_sem.at[i],
            device_id=(view, tile_of(i)), device_id_type=pl.DeviceIdType.MESH,
        )

    def points_copy(k, i):
        at = k * tiles + i
        return pltpu.make_async_remote_copy(
            src_ref=send_ref.at[view_of(k) * tiles + tile_of(i)], dst_ref=got.at[at],
            send_sem=send_sem.at[at], recv_sem=recv_sem.at[at],
            device_id=(view, tile_of(i)), device_id_type=pl.DeviceIdType.MESH,
        )

    def dense_copy(k):
        return pltpu.make_async_remote_copy(
            src_ref=dense_send.at[k], dst_ref=dense_got.at[k],
            send_sem=dense_send_sem.at[k], recv_sem=dense_recv_sem.at[k],
            device_id=(view_of(k), tile), device_id_type=pl.DeviceIdType.MESH,
        )

    def hist_copy(k):
        return pltpu.make_async_remote_copy(
            src_ref=hist, dst_ref=hist_got.at[k],
            send_sem=hist_send_sem.at[k], recv_sem=hist_recv_sem.at[k],
            device_id=(view_of(k), tile), device_id_type=pl.DeviceIdType.MESH,
        )

    @pl.loop(1, tiles)
    def _(i):
        meta_copy(i).start()

    @pl.loop(0, views)
    def _(k):
        @pl.loop(1, tiles)
        def _(i):
            points_copy(k, i).start()

    hi_rows = lax.broadcasted_iota(jnp.int32, (HI, points), 0)
    hi_ids = jnp.where(hi_rows < half, 2 * hi_rows, 2 * hi_rows - (HI - 1)).astype(jnp.float32)
    lo_ids = lax.broadcasted_iota(jnp.int32, (LO, points), 0).astype(jnp.float32)
    lanes = q * 128
    hist_hi = lax.broadcasted_iota(jnp.int32, (hist.shape[0], lanes), 0).astype(jnp.float32)
    hist_lo = lax.broadcasted_iota(jnp.int32, (128, lanes), 0).astype(jnp.float32)
    row_ids = lax.broadcasted_iota(jnp.int32, (blocks_dev, slots), 0).astype(jnp.float32)

    @pl.loop(0, tiles)
    def _(j):
        pltpu.make_async_copy(got_meta.at[j], got_meta.at[j], meta_recv_sem.at[j]).wait()
        meta = got_meta[j]
        storage = jnp.concatenate([meta[views + k : views + k + 1, :] for k in range(q)], axis=1)
        counts = jnp.concatenate(
            [meta[views + q + k : views + q + k + 1, :] for k in range(q)], axis=1
        )
        s_hi = jnp.floor(storage * (1.0 / 128))
        s_lo = storage - s_hi * 128.0
        a = jnp.where(s_hi == hist_hi, counts, 0.0).astype(jnp.bfloat16)
        b = jnp.where(s_lo == hist_lo, 1.0, 0.0).astype(jnp.bfloat16)
        hist[...] += lax.dot_general(a, b, NT, preferred_element_type=jnp.float32)

    def one_source(k, j):
        at = k * tiles + j
        pltpu.make_async_copy(got.at[at], got.at[at], recv_sem.at[at]).wait()
        block[...] = got[at].astype(jnp.float32)
        voxel = block[CH * cap : (CH + 1) * cap, :] + float(VOX // 2)
        high = jnp.floor(voxel * (1.0 / LO))
        low = voxel - high * float(LO)
        for s in range(cap):
            mask = jnp.broadcast_to(high[s : s + 1, :], (HI, points)) == hi_ids
            a = jnp.concatenate(
                [
                    jnp.where(
                        mask,
                        jnp.broadcast_to(block[c * cap + s : c * cap + s + 1, :], (HI, points)),
                        0.0,
                    )
                    for c in range(CH)
                ],
                axis=0,
            ).astype(jnp.bfloat16)
            b = jnp.where(
                jnp.broadcast_to(low[s : s + 1, :], (LO, points)) == lo_ids, 1.0, 0.0
            ).astype(jnp.bfloat16)
            parts[pl.ds(j * cap + s, rows, stride=slots), :] = lax.dot_general(
                a, b, NT, preferred_element_type=jnp.float32
            )

    @pl.loop(0, views)
    def _(k):
        @pl.loop(0, tiles)
        def _(j):
            one_source(k, j)

        @pl.when(k == 0)
        def _():
            @pl.loop(0, views - 1)
            def _(v):
                hist_copy(v).start()

        row = jnp.concatenate(
            [got_meta[j, pl.ds(k, 1), 0:cap] for j in range(tiles)], axis=1
        )
        hot = jnp.where(row == row_ids, 1.0, 0.0).astype(jnp.bfloat16)
        for c in range(CH):
            for h in range(half):
                pair = [
                    jnp.dot(
                        hot,
                        parts[r * slots : (r + 1) * slots, :].astype(jnp.bfloat16),
                        preferred_element_type=jnp.float32,
                    )
                    for r in (c * HI + h, c * HI + half + h)
                ]
                acc[c * half + h] = jnp.concatenate(pair, axis=1)

        @pl.when(k < views - 1)
        def _():
            dense_send[k] = acc[...].astype(jnp.bfloat16)
            dense_copy(k).start()

    @pl.loop(0, views - 1)
    def _(k):
        dense_copy(k).wait_recv()
        acc[...] += dense_got[k].astype(jnp.float32)

    for h in range(half):
        at = slice(h * 2 * LO, (h + 1) * 2 * LO)
        divisor = jnp.maximum(acc[h], 1.0)
        tsdf_ref[:, at] = acc[half + h] / divisor
        for c in range(3):
            color_ref[c, :, at] = acc[(2 + c) * half + h] / divisor

    total = hist[...]
    for k in range(views - 1):
        hist_copy(k).wait_recv()
        total += hist_got[k]
    counts_ref[...] = total.astype(jnp.int32)

    @pl.loop(1, tiles)
    def _(i):
        meta_copy(i).wait_send()

    @pl.loop(0, views)
    def _(k):
        @pl.loop(1, tiles)
        def _(i):
            points_copy(k, i).wait_send()

    @pl.loop(0, views - 1)
    def _(k):
        dense_copy(k).wait_send()
        hist_copy(k).wait_send()


def on_device(tiles, sdf_value, weight, color, voxel_index, valid, list_count, list_key, owner_slot):
    lists, points = sdf_value.shape
    n = lax.axis_size(AXES)
    blocks_all = owner_slot.shape[0]
    blocks_dev = blocks_all // n
    cap = 4 * lists // n
    q = -(-lists // 128)
    views = n // tiles

    position = jnp.arange(points, dtype=jnp.int32)
    live_points = jnp.sum(
        ((position[None, :] < list_count[:, None]) & (valid == 1)).astype(jnp.int32), axis=1
    )
    key_match = list_key[:, None] == jnp.arange(blocks_all, dtype=jnp.int32)[None, :]
    storage = jnp.sum(jnp.where(key_match, owner_slot[None, :], 0), axis=1)
    owner = storage // blocks_dev
    row = storage % blocks_dev
    ids = jnp.arange(lists, dtype=jnp.int32)
    arrival = jnp.sum(
        ((owner[:, None] == owner[None, :]) & (ids[None, :] < ids[:, None])).astype(jnp.int32), axis=1
    )
    slot = owner * cap + arrival
    slot_row = (
        jnp.max(
            jnp.where(
                slot[None, :] == jnp.arange(n * cap, dtype=jnp.int32)[:, None], row[None, :], -1
            ),
            axis=1,
        )
        .astype(jnp.float32)
        .reshape(n, 1, cap)
    )
    slot_row = jnp.pad(slot_row, ((0, 0), (0, 0), (0, 128 - cap)), constant_values=-1.0)

    def lane_rows(x):
        x = jnp.pad(x.astype(jnp.float32), (0, q * 128 - lists)).reshape(1, q, 128)
        return jnp.broadcast_to(x, (tiles, q, 128))

    steps = jnp.arange(views - 1, -1, -1, dtype=jnp.int32)
    my_view = lax.axis_index("view")
    if views & (views - 1):
        order = (my_view + steps) % views
    else:
        order = my_view ^ steps
    by_view = jnp.take(slot_row.reshape(views, tiles, 128), order, axis=0)
    by_tile = jnp.swapaxes(by_view, 0, 1)
    meta_rows = -(-(views + 2 * q) // 8) * 8
    meta = jnp.concatenate(
        [
            by_tile,
            lane_rows(storage),
            lane_rows(live_points),
            jnp.zeros((tiles, meta_rows - views - 2 * q, 128), jnp.float32),
        ],
        axis=1,
    )
    send = pl.pallas_call(
        functools.partial(pack_kernel, n, cap),
        out_shape=jax.ShapeDtypeStruct((n, (CH + 1) * cap, points), jnp.bfloat16),
        in_specs=[pl.BlockSpec(memory_space=pltpu.VMEM)] * 7,
        out_specs=pl.BlockSpec(memory_space=pltpu.VMEM),
    )(slot[None, :], list_count[:, None], sdf_value, weight, color, voxel_index, valid)

    rows = CH * HI
    tsdf, joined, counts = pl.pallas_call(
        functools.partial(join_kernel, views, tiles, cap, q),
        out_shape=(
            jax.ShapeDtypeStruct((blocks_dev, VOX), jnp.float32),
            jax.ShapeDtypeStruct((3, blocks_dev, VOX), jnp.float32),
            jax.ShapeDtypeStruct((blocks_all // 128, 128), jnp.int32),
        ),
        in_specs=[pl.BlockSpec(memory_space=pl.ANY)] * 2,
        out_specs=(pl.BlockSpec(memory_space=pltpu.VMEM),) * 3,
        scratch_shapes=[
            pltpu.VMEM((n, (CH + 1) * cap, points), jnp.bfloat16),
            pltpu.VMEM((tiles, meta_rows, 128), jnp.float32),
            pltpu.VMEM(((CH + 1) * cap, points), jnp.float32),
            pltpu.VMEM((rows * tiles * cap, LO), jnp.float32),
            pltpu.VMEM((rows // 2, blocks_dev, 2 * LO), jnp.float32),
            pltpu.VMEM((views - 1, rows // 2, blocks_dev, 2 * LO), jnp.bfloat16),
            pltpu.VMEM((views - 1, rows // 2, blocks_dev, 2 * LO), jnp.bfloat16),
            pltpu.VMEM((blocks_all // 128, 128), jnp.float32),
            pltpu.VMEM((views - 1, blocks_all // 128, 128), jnp.float32),
            pltpu.SemaphoreType.DMA((n,)),
            pltpu.SemaphoreType.DMA((n,)),
            pltpu.SemaphoreType.DMA((tiles,)),
            pltpu.SemaphoreType.DMA((tiles,)),
            pltpu.SemaphoreType.DMA((views - 1,)),
            pltpu.SemaphoreType.DMA((views - 1,)),
            pltpu.SemaphoreType.DMA((views - 1,)),
            pltpu.SemaphoreType.DMA((views - 1,)),
        ],
        compiler_params=pltpu.CompilerParams(collective_id=0, has_side_effects=True),
    )(send, meta)
    return tsdf, jnp.swapaxes(joined, 0, 1), counts.reshape(blocks_all)


def solution(mesh):
    return jax.shard_map(
        functools.partial(on_device, mesh.shape["tile"]),
        mesh=mesh,
        in_specs=(
            P(AXES, None),
            P(AXES, None),
            P(None, AXES, None),
            P(AXES, None),
            P(AXES, None),
            P(AXES),
            P(AXES),
            P(),
        ),
        out_specs=(P(AXES, None), P(AXES, None, None), P()),
        check_vma=False,
    )
```

```python
import functools

import jax
import jax.numpy as jnp
from jax import lax
from jax.experimental import pallas as pl
from jax.experimental.pallas import tpu as pltpu
from jax.sharding import PartitionSpec as P

VOX = 512
HI = 8
LO = VOX // HI
CH = 5
AXES = ("view", "tile")
NT = (((1,), (1,)), ((), ()))
TN = (((0,), (0,)), ((), ()))
NN = (((1,), (0,)), ((), ()))


def finish_kernel(sums_ref, hist_ref, tsdf_ref, color_ref, counts_ref):
    half = HI // 2
    for h in range(half):
        at = slice(h * 2 * LO, (h + 1) * 2 * LO)
        divisor = jnp.maximum(sums_ref[h], 1.0)
        tsdf_ref[:, at] = sums_ref[half + h] / divisor
        for c in range(3):
            color_ref[c, :, at] = sums_ref[(2 + c) * half + h] / divisor
    counts_ref[...] = hist_ref[...].astype(jnp.int32)


def join_kernel(
    views, tiles, cap, q, key_ref, owner_ref, count_ref, sdf_ref, weight_ref, color_ref,
    voxel_ref, valid_ref, acc, total_ref,
    send_ref, meta_ref, values, got, got_meta, block, parts, dense_send, dense_got, hist, hist_got,
    send_sem, recv_sem, meta_send_sem, meta_recv_sem,
    dense_send_sem, dense_recv_sem, hist_send_sem, hist_recv_sem,
):
    view = lax.axis_index("view")
    tile = lax.axis_index("tile")
    points = send_ref.shape[-1]
    lists = sdf_ref.shape[0]
    blocks_dev = acc.shape[1]
    rows = CH * HI
    slots = tiles * cap
    pitch = slots + 8
    half = HI // 2

    def view_of(k):
        step = views - 1 - k
        if views & (views - 1):
            return lax.rem(view + step, views)
        partner = 0
        bit = 1
        while bit < views:
            mine = (view // bit) % 2
            flip = (step // bit) % 2
            partner = partner + bit * (mine + flip - 2 * mine * flip)
            bit *= 2
        return partner

    def tile_of(i):
        return lax.rem(tile + i, tiles)

    barrier = pltpu.get_barrier_semaphore()

    @pl.loop(1, tiles)
    def _(i):
        pl.semaphore_signal(
            barrier, inc=1, device_id=(view, tile_of(i)), device_id_type=pl.DeviceIdType.MESH
        )

    @pl.loop(0, views - 1)
    def _(k):
        pl.semaphore_signal(
            barrier, inc=1, device_id=(view_of(k), tile), device_id_type=pl.DeviceIdType.MESH
        )

    def own_copy(k):
        return pltpu.make_async_copy(
            send_ref.at[k * tiles + tile], got.at[k * tiles], recv_sem.at[k * tiles]
        )

    bf16, f32 = jnp.bfloat16, jnp.float32

    def iota(shape, dim):
        return lax.broadcasted_iota(jnp.int32, shape, dim).astype(f32)

    def dot(a, b, dims):
        return lax.dot_general(a, b, dims, preferred_element_type=f32)

    key = key_ref[...].astype(f32)
    key_hi = jnp.floor(key * (1.0 / 128))
    key_lo = key - key_hi * 128.0
    table = owner_ref[...].astype(f32)
    table_hi = jnp.floor(table * (1.0 / 64))
    table_lo = table - table_hi * 64.0
    hot_hi = jnp.where(key_hi == iota((table.shape[0], lists), 0), 1.0, 0.0).astype(bf16)
    found = 64.0 * dot(table_hi.astype(bf16), hot_hi, TN) + dot(table_lo.astype(bf16), hot_hi, TN)
    storage = jnp.sum(
        jnp.where(key_lo == iota((128, lists), 0), found, 0.0), axis=0, keepdims=True
    )
    owner = jnp.floor((storage + 0.5) * (1.0 / blocks_dev))
    block_row = storage - owner * blocks_dev
    is_owner = owner == iota((views * tiles, lists), 0)
    before = jnp.where(iota((lists, lists), 0) < iota((lists, lists), 1), 1.0, 0.0).astype(bf16)
    earlier = dot(jnp.where(is_owner, 1.0, 0.0).astype(bf16), before, NN)
    arrival = jnp.sum(jnp.where(is_owner, earlier, 0.0), axis=0, keepdims=True)
    slot = owner * cap + arrival

    diagonal = iota((lists, lists), 0) == iota((lists, lists), 1)
    list_count = dot(
        jnp.where(diagonal, count_ref[...].astype(f32), 0.0).astype(bf16),
        jnp.ones((lists, points), bf16), NN,
    )
    live = (iota((lists, points), 1) < list_count) & (valid_ref[...] == 1)
    scaled = jnp.where(live, weight_ref[...], 0.0)
    values[0] = scaled.astype(bf16)
    values[1] = (scaled * sdf_ref[...]).astype(bf16)
    for c in range(3):
        values[2 + c] = (scaled * color_ref[c]).astype(bf16)
    values[CH] = (voxel_ref[...] - VOX // 2).astype(f32).astype(bf16)
    live_count = dot(jnp.ones((8, points), bf16), jnp.where(live, 1.0, 0.0).astype(bf16), NT)[0:1]

    meta_ref[...] = jnp.zeros_like(meta_ref)
    for j in range(q):
        at = slice(j * 128, min(lists, (j + 1) * 128))
        for t in range(tiles):
            meta_ref[t, views + j : views + j + 1, 0 : at.stop - at.start] = storage[:, at]
            meta_ref[t, views + q + j : views + q + j + 1, 0 : at.stop - at.start] = live_count[:, at]
    row_code = jnp.broadcast_to(block_row + 1.0, (8, lists)).astype(bf16)

    for k in range(views):
        first = (view_of(k) * slots).astype(f32)
        placement = jnp.where(iota((slots, lists), 0) + first == slot, 1.0, 0.0).astype(bf16)
        slot_rows = dot(row_code, placement, NT) - 1.0
        for t in range(tiles):
            meta_ref[t, k : k + 1, 0:cap] = slot_rows[0:1, t * cap : (t + 1) * cap]
        for c in range(CH + 1):
            placed = dot(placement, values[c], NN).astype(bf16)
            for t in range(tiles):
                send_ref[k * tiles + t, c * cap : (c + 1) * cap, :] = placed[t * cap : (t + 1) * cap]
    hist[...] = jnp.zeros_like(hist)
    pl.semaphore_wait(barrier, tiles - 1 + views - 1)

    own_meta = pltpu.make_async_copy(meta_ref.at[tile], got_meta.at[0], meta_recv_sem.at[0])
    own_meta.start()

    @pl.loop(0, views)
    def _(k):
        own_copy(k).start()

    def meta_copy(i):
        return pltpu.make_async_remote_copy(
            src_ref=meta_ref.at[tile_of(i)], dst_ref=got_meta.at[i],
            send_sem=meta_send_sem.at[i], recv_sem=meta_recv_sem.at[i],
            device_id=(view, tile_of(i)), device_id_type=pl.DeviceIdType.MESH,
        )

    def points_copy(k, i):
        at = k * tiles + i
        return pltpu.make_async_remote_copy(
            src_ref=send_ref.at[k * tiles + tile_of(i)], dst_ref=got.at[at],
            send_sem=send_sem.at[at], recv_sem=recv_sem.at[at],
            device_id=(view, tile_of(i)), device_id_type=pl.DeviceIdType.MESH,
        )

    def dense_copy(k):
        return pltpu.make_async_remote_copy(
            src_ref=dense_send.at[k], dst_ref=dense_got.at[k],
            send_sem=dense_send_sem.at[k], recv_sem=dense_recv_sem.at[k],
            device_id=(view_of(k), tile), device_id_type=pl.DeviceIdType.MESH,
        )

    def hist_copy(k):
        return pltpu.make_async_remote_copy(
            src_ref=hist, dst_ref=hist_got.at[k],
            send_sem=hist_send_sem.at[k], recv_sem=hist_recv_sem.at[k],
            device_id=(view_of(k), tile), device_id_type=pl.DeviceIdType.MESH,
        )

    @pl.loop(1, tiles)
    def _(i):
        meta_copy(i).start()

    @pl.loop(0, views)
    def _(k):
        @pl.loop(1, tiles)
        def _(i):
            points_copy(k, i).start()

    hi_rows = lax.broadcasted_iota(jnp.int32, (HI, points), 0)
    hi_ids = jnp.where(hi_rows < half, 2 * hi_rows, 2 * hi_rows - (HI - 1)).astype(jnp.float32)
    lo_ids = lax.broadcasted_iota(jnp.int32, (LO, points), 0).astype(jnp.float32)
    lanes = q * 128
    hist_hi = lax.broadcasted_iota(jnp.int32, (hist.shape[0], lanes), 0).astype(jnp.float32)
    hist_lo = lax.broadcasted_iota(jnp.int32, (128, lanes), 0).astype(jnp.float32)
    row_ids = lax.broadcasted_iota(jnp.int32, (blocks_dev, slots), 0).astype(jnp.float32)

    @pl.loop(0, tiles)
    def _(j):
        pltpu.make_async_copy(got_meta.at[j], got_meta.at[j], meta_recv_sem.at[j]).wait()
        meta = got_meta[j]
        storage = jnp.concatenate([meta[views + k : views + k + 1, :] for k in range(q)], axis=1)
        counts = jnp.concatenate(
            [meta[views + q + k : views + q + k + 1, :] for k in range(q)], axis=1
        )
        s_hi = jnp.floor(storage * (1.0 / 128))
        s_lo = storage - s_hi * 128.0
        a = jnp.where(s_hi == hist_hi, counts, 0.0).astype(jnp.bfloat16)
        b = jnp.where(s_lo == hist_lo, 1.0, 0.0).astype(jnp.bfloat16)
        hist[...] += lax.dot_general(a, b, NT, preferred_element_type=jnp.float32)

    def one_source(k, j):
        at = k * tiles + j
        pltpu.make_async_copy(got.at[at], got.at[at], recv_sem.at[at]).wait()
        block[...] = got[at].astype(jnp.float32)
        voxel = block[CH * cap : (CH + 1) * cap, :] + float(VOX // 2)
        high = jnp.floor(voxel * (1.0 / LO))
        low = voxel - high * float(LO)
        for s in range(cap):
            mask = jnp.broadcast_to(high[s : s + 1, :], (HI, points)) == hi_ids
            a = jnp.concatenate(
                [
                    jnp.where(
                        mask,
                        jnp.broadcast_to(block[c * cap + s : c * cap + s + 1, :], (HI, points)),
                        0.0,
                    )
                    for c in range(CH)
                ],
                axis=0,
            ).astype(jnp.bfloat16)
            b = jnp.where(
                jnp.broadcast_to(low[s : s + 1, :], (LO, points)) == lo_ids, 1.0, 0.0
            ).astype(jnp.bfloat16)
            parts[pl.ds(j * cap + s, rows, stride=pitch), :] = lax.dot_general(
                a, b, NT, preferred_element_type=jnp.float32
            )

    @pl.loop(0, views)
    def _(k):
        @pl.loop(0, tiles)
        def _(j):
            one_source(k, j)

        @pl.when(k == 0)
        def _():
            @pl.loop(0, views - 1)
            def _(v):
                hist_copy(v).start()

        row = jnp.concatenate(
            [got_meta[j, pl.ds(k, 1), 0:cap] for j in range(tiles)], axis=1
        )
        hot = jnp.where(row == row_ids, 1.0, 0.0).astype(jnp.bfloat16)
        for c in range(CH):
            for h in range(half):
                pair = [
                    jnp.dot(
                        hot,
                        parts[r * pitch : r * pitch + slots, :].astype(jnp.bfloat16),
                        preferred_element_type=jnp.float32,
                    )
                    for r in (c * HI + h, c * HI + half + h)
                ]
                acc[c * half + h] = jnp.concatenate(pair, axis=1)

        @pl.when(k < views - 1)
        def _():
            dense_send[k] = acc[...].astype(jnp.bfloat16)
            dense_copy(k).start()

    @pl.loop(0, views - 1)
    def _(k):
        dense_copy(k).wait_recv()
        acc[...] += dense_got[k].astype(jnp.float32)

    total = hist[...]
    for k in range(views - 1):
        hist_copy(k).wait_recv()
        total += hist_got[k]
    total_ref[...] = total

    @pl.loop(1, tiles)
    def _(i):
        meta_copy(i).wait_send()

    @pl.loop(0, views)
    def _(k):
        @pl.loop(1, tiles)
        def _(i):
            points_copy(k, i).wait_send()

    @pl.loop(0, views - 1)
    def _(k):
        dense_copy(k).wait_send()
        hist_copy(k).wait_send()


def on_device(tiles, sdf_value, weight, color, voxel_index, valid, list_count, list_key, owner_slot):
    lists, points = sdf_value.shape
    n = lax.axis_size(AXES)
    blocks_all = owner_slot.shape[0]
    blocks_dev = blocks_all // n
    cap = 4 * lists // n
    q = -(-lists // 128)
    views = n // tiles

    meta_rows = -(-(views + 2 * q) // 8) * 8
    payload = (n, (CH + 1) * cap, points)
    wide = (blocks_all // 128, 128)
    rows = CH * HI
    vmem = pl.BlockSpec(memory_space=pltpu.VMEM)
    sums, total = pl.pallas_call(
        functools.partial(join_kernel, views, tiles, cap, q),
        out_shape=(
            jax.ShapeDtypeStruct((rows // 2, blocks_dev, 2 * LO), jnp.float32),
            jax.ShapeDtypeStruct(wide, jnp.float32),
        ),
        in_specs=[vmem] * 8,
        out_specs=(vmem,) * 2,
        scratch_shapes=[
            pltpu.VMEM(payload, jnp.bfloat16),
            pltpu.VMEM((tiles, meta_rows, 128), jnp.float32),
            pltpu.VMEM((CH + 1, lists, points), jnp.bfloat16),
            pltpu.VMEM(payload, jnp.bfloat16),
            pltpu.VMEM((tiles, meta_rows, 128), jnp.float32),
            pltpu.VMEM(((CH + 1) * cap, points), jnp.float32),
            pltpu.VMEM((rows * (tiles * cap + 8), LO), jnp.float32),
            pltpu.VMEM((views - 1, rows // 2, blocks_dev, 2 * LO), jnp.bfloat16),
            pltpu.VMEM((views - 1, rows // 2, blocks_dev, 2 * LO), jnp.bfloat16),
            pltpu.VMEM((blocks_all // 128, 128), jnp.float32),
            pltpu.VMEM((views - 1, blocks_all // 128, 128), jnp.float32),
            pltpu.SemaphoreType.DMA((n,)),
            pltpu.SemaphoreType.DMA((n,)),
            pltpu.SemaphoreType.DMA((tiles,)),
            pltpu.SemaphoreType.DMA((tiles,)),
            pltpu.SemaphoreType.DMA((views - 1,)),
            pltpu.SemaphoreType.DMA((views - 1,)),
            pltpu.SemaphoreType.DMA((views - 1,)),
            pltpu.SemaphoreType.DMA((views - 1,)),
        ],
        compiler_params=pltpu.CompilerParams(collective_id=0, has_side_effects=True),
    )(
        list_key.reshape(1, lists), owner_slot.reshape(wide), list_count.reshape(1, lists),
        sdf_value, weight, color, voxel_index, valid,
    )
    tsdf, joined, counts = pl.pallas_call(
        finish_kernel,
        out_shape=(
            jax.ShapeDtypeStruct((blocks_dev, VOX), jnp.float32),
            jax.ShapeDtypeStruct((3, blocks_dev, VOX), jnp.float32),
            jax.ShapeDtypeStruct(wide, jnp.int32),
        ),
        in_specs=[vmem] * 2,
        out_specs=(vmem,) * 3,
    )(sums, total)
    return tsdf, jnp.swapaxes(joined, 0, 1), counts.reshape(blocks_all)


def solution(mesh):
    return jax.shard_map(
        functools.partial(on_device, mesh.shape["tile"]),
        mesh=mesh,
        in_specs=(
            P(AXES, None),
            P(AXES, None),
            P(None, AXES, None),
            P(AXES, None),
            P(AXES, None),
            P(AXES),
            P(AXES),
            P(),
        ),
        out_specs=(P(AXES, None), P(AXES, None, None), P()),
        check_vma=False,
    )
```

```python
import functools

import jax
import jax.numpy as jnp
from jax import lax
from jax.experimental import pallas as pl
from jax.experimental.pallas import tpu as pltpu
from jax.sharding import PartitionSpec as P

VOX = 512
HI = 8
LO = VOX // HI
CH = 5
AXES = ("view", "tile")
NT = (((1,), (1,)), ((), ()))
TN = (((0,), (0,)), ((), ()))
NN = (((1,), (0,)), ((), ()))


def finish_kernel(sums_ref, hist_ref, tsdf_ref, color_ref, counts_ref):
    half = HI // 2
    for h in range(half):
        at = slice(h * 2 * LO, (h + 1) * 2 * LO)
        divisor = jnp.maximum(sums_ref[h], 1.0)
        tsdf_ref[:, at] = sums_ref[half + h] / divisor
        for c in range(3):
            color_ref[c, :, at] = sums_ref[(2 + c) * half + h] / divisor
    counts_ref[...] = hist_ref[...].astype(jnp.int32)


def join_kernel(
    views, tiles, cap, q, key_ref, owner_ref, count_ref, sdf_ref, weight_ref, color_ref,
    voxel_ref, valid_ref, acc, total_ref,
    send_ref, meta_ref, values, got, got_meta, block, parts, dense_send, dense_got, hist, hist_got,
    send_sem, recv_sem, meta_send_sem, meta_recv_sem,
    dense_send_sem, dense_recv_sem, hist_send_sem, hist_recv_sem,
):
    view = lax.axis_index("view")
    tile = lax.axis_index("tile")
    points = send_ref.shape[-1]
    lists = sdf_ref.shape[0]
    blocks_dev = acc.shape[1]
    rows = CH * HI
    slots = tiles * cap
    pitch = slots + 8
    half = HI // 2

    def view_of(k):
        step = views - 1 - k
        if views & (views - 1):
            return lax.rem(view + step, views)
        partner = 0
        bit = 1
        while bit < views:
            mine = (view // bit) % 2
            flip = (step // bit) % 2
            partner = partner + bit * (mine + flip - 2 * mine * flip)
            bit *= 2
        return partner

    def tile_of(i):
        return lax.rem(tile + i, tiles)

    barrier = pltpu.get_barrier_semaphore()

    @pl.loop(1, tiles)
    def _(i):
        pl.semaphore_signal(
            barrier, inc=1, device_id=(view, tile_of(i)), device_id_type=pl.DeviceIdType.MESH
        )

    @pl.loop(0, views - 1)
    def _(k):
        pl.semaphore_signal(
            barrier, inc=1, device_id=(view_of(k), tile), device_id_type=pl.DeviceIdType.MESH
        )

    def own_copy(k):
        return pltpu.make_async_copy(
            send_ref.at[k * tiles + tile], got.at[k * tiles], recv_sem.at[k * tiles]
        )

    bf16, f32 = jnp.bfloat16, jnp.float32

    def iota(shape, dim):
        return lax.broadcasted_iota(jnp.int32, shape, dim).astype(f32)

    def dot(a, b, dims):
        return lax.dot_general(a, b, dims, preferred_element_type=f32)

    key = key_ref[...].astype(f32)
    key_hi = jnp.floor(key * (1.0 / 128))
    key_lo = key - key_hi * 128.0
    table = owner_ref[...].astype(f32)
    table_hi = jnp.floor(table * (1.0 / 64))
    table_lo = table - table_hi * 64.0
    hot_hi = jnp.where(key_hi == iota((table.shape[0], lists), 0), 1.0, 0.0).astype(bf16)
    found = 64.0 * dot(table_hi.astype(bf16), hot_hi, TN) + dot(table_lo.astype(bf16), hot_hi, TN)
    storage = jnp.sum(
        jnp.where(key_lo == iota((128, lists), 0), found, 0.0), axis=0, keepdims=True
    )
    owner = jnp.floor((storage + 0.5) * (1.0 / blocks_dev))
    block_row = storage - owner * blocks_dev
    is_owner = owner == iota((views * tiles, lists), 0)
    before = jnp.where(iota((lists, lists), 0) < iota((lists, lists), 1), 1.0, 0.0).astype(bf16)
    earlier = dot(jnp.where(is_owner, 1.0, 0.0).astype(bf16), before, NN)
    arrival = jnp.sum(jnp.where(is_owner, earlier, 0.0), axis=0, keepdims=True)
    slot = owner * cap + arrival

    diagonal = iota((lists, lists), 0) == iota((lists, lists), 1)
    list_count = dot(
        jnp.where(diagonal, count_ref[...].astype(f32), 0.0).astype(bf16),
        jnp.ones((lists, points), bf16), NN,
    )
    live = (iota((lists, points), 1) < list_count) & (valid_ref[...] == 1)
    scaled = jnp.where(live, weight_ref[...], 0.0)
    values[0] = scaled.astype(bf16)
    values[1] = (scaled * sdf_ref[...]).astype(bf16)
    for c in range(3):
        values[2 + c] = (scaled * color_ref[c]).astype(bf16)
    values[CH] = (voxel_ref[...] - VOX // 2).astype(f32).astype(bf16)
    live_count = dot(jnp.ones((8, points), bf16), jnp.where(live, 1.0, 0.0).astype(bf16), NT)[0:1]

    meta_ref[...] = jnp.zeros_like(meta_ref)
    for j in range(q):
        at = slice(j * 128, min(lists, (j + 1) * 128))
        for t in range(tiles):
            meta_ref[t, views + j : views + j + 1, 0 : at.stop - at.start] = storage[:, at]
            meta_ref[t, views + q + j : views + q + j + 1, 0 : at.stop - at.start] = live_count[:, at]
    row_code = jnp.broadcast_to(block_row + 1.0, (8, lists)).astype(bf16)

    def placement_of(k):
        first = (view_of(k) * slots).astype(f32)
        return jnp.where(iota((slots, lists), 0) + first == slot, 1.0, 0.0).astype(bf16)

    for k in range(views):
        slot_rows = dot(row_code, placement_of(k), NT) - 1.0
        for t in range(tiles):
            meta_ref[t, k : k + 1, 0:cap] = slot_rows[0:1, t * cap : (t + 1) * cap]

    def meta_copy(i):
        return pltpu.make_async_remote_copy(
            src_ref=meta_ref.at[tile_of(i)], dst_ref=got_meta.at[i],
            send_sem=meta_send_sem.at[i], recv_sem=meta_recv_sem.at[i],
            device_id=(view, tile_of(i)), device_id_type=pl.DeviceIdType.MESH,
        )

    def points_copy(k, i):
        at = k * tiles + i
        return pltpu.make_async_remote_copy(
            src_ref=send_ref.at[k * tiles + tile_of(i)], dst_ref=got.at[at],
            send_sem=send_sem.at[at], recv_sem=recv_sem.at[at],
            device_id=(view, tile_of(i)), device_id_type=pl.DeviceIdType.MESH,
        )

    def dense_copy(k):
        return pltpu.make_async_remote_copy(
            src_ref=dense_send.at[k], dst_ref=dense_got.at[k],
            send_sem=dense_send_sem.at[k], recv_sem=dense_recv_sem.at[k],
            device_id=(view_of(k), tile), device_id_type=pl.DeviceIdType.MESH,
        )

    relaying = views == 4
    outer = 1 - ((view + 1) // 2) % 2 if relaying else 0
    relay_slot = views - 1

    def relay_copy():
        return pltpu.make_async_remote_copy(
            src_ref=dense_send.at[0], dst_ref=dense_got.at[relay_slot],
            send_sem=dense_send_sem.at[0], recv_sem=dense_recv_sem.at[relay_slot],
            device_id=(view_of(views - 2), tile), device_id_type=pl.DeviceIdType.MESH,
        )

    def hist_copy(k):
        return pltpu.make_async_remote_copy(
            src_ref=hist, dst_ref=hist_got.at[k],
            send_sem=hist_send_sem.at[k], recv_sem=hist_recv_sem.at[k],
            device_id=(view_of(k), tile), device_id_type=pl.DeviceIdType.MESH,
        )

    def send_parcels(k):
        own_copy(k).start()

        @pl.loop(1, tiles)
        def _(i):
            points_copy(k, i).start()

    hist[...] = jnp.zeros_like(hist)
    for k in range(views):
        placement = placement_of(k)
        for c in range(CH + 1):
            placed = dot(placement, values[c], NN).astype(bf16)
            for t in range(tiles):
                send_ref[k * tiles + t, c * cap : (c + 1) * cap, :] = placed[t * cap : (t + 1) * cap]
        if k == 0:
            pl.semaphore_wait(barrier, tiles - 1 + views - 1)
            own_meta = pltpu.make_async_copy(
                meta_ref.at[tile], got_meta.at[0], meta_recv_sem.at[0]
            )
            own_meta.start()

            @pl.loop(1, tiles)
            def _(i):
                meta_copy(i).start()

        else:
            send_parcels(k - 1)
    send_parcels(views - 1)

    hi_rows = lax.broadcasted_iota(jnp.int32, (HI, points), 0)
    hi_ids = jnp.where(hi_rows < half, 2 * hi_rows, 2 * hi_rows - (HI - 1)).astype(jnp.float32)
    lo_ids = lax.broadcasted_iota(jnp.int32, (LO, points), 0).astype(jnp.float32)
    lanes = q * 128
    hist_hi = lax.broadcasted_iota(jnp.int32, (hist.shape[0], lanes), 0).astype(jnp.float32)
    hist_lo = lax.broadcasted_iota(jnp.int32, (128, lanes), 0).astype(jnp.float32)
    row_ids = lax.broadcasted_iota(jnp.int32, (blocks_dev, slots), 0).astype(jnp.float32)

    @pl.loop(0, tiles)
    def _(j):
        pltpu.make_async_copy(got_meta.at[j], got_meta.at[j], meta_recv_sem.at[j]).wait()
        meta = got_meta[j]
        storage = jnp.concatenate([meta[views + k : views + k + 1, :] for k in range(q)], axis=1)
        counts = jnp.concatenate(
            [meta[views + q + k : views + q + k + 1, :] for k in range(q)], axis=1
        )
        s_hi = jnp.floor(storage * (1.0 / 128))
        s_lo = storage - s_hi * 128.0
        a = jnp.where(s_hi == hist_hi, counts, 0.0).astype(jnp.bfloat16)
        b = jnp.where(s_lo == hist_lo, 1.0, 0.0).astype(jnp.bfloat16)
        hist[...] += lax.dot_general(a, b, NT, preferred_element_type=jnp.float32)

    def one_source(k, j):
        at = k * tiles + j
        pltpu.make_async_copy(got.at[at], got.at[at], recv_sem.at[at]).wait()
        block[...] = got[at].astype(jnp.float32)
        voxel = block[CH * cap : (CH + 1) * cap, :] + float(VOX // 2)
        high = jnp.floor(voxel * (1.0 / LO))
        low = voxel - high * float(LO)
        for s in range(cap):
            mask = jnp.broadcast_to(high[s : s + 1, :], (HI, points)) == hi_ids
            a = jnp.concatenate(
                [
                    jnp.where(
                        mask,
                        jnp.broadcast_to(block[c * cap + s : c * cap + s + 1, :], (HI, points)),
                        0.0,
                    )
                    for c in range(CH)
                ],
                axis=0,
            ).astype(jnp.bfloat16)
            b = jnp.where(
                jnp.broadcast_to(low[s : s + 1, :], (LO, points)) == lo_ids, 1.0, 0.0
            ).astype(jnp.bfloat16)
            parts[pl.ds(j * cap + s, rows, stride=pitch), :] = lax.dot_general(
                a, b, NT, preferred_element_type=jnp.float32
            )

    @pl.loop(0, views)
    def _(k):
        @pl.loop(0, tiles)
        def _(j):
            one_source(k, j)

        @pl.when(k == 0)
        def _():
            @pl.loop(0, views - 1)
            def _(v):
                hist_copy(v).start()

        row = jnp.concatenate(
            [got_meta[j, pl.ds(k, 1), 0:cap] for j in range(tiles)], axis=1
        )
        hot = jnp.where(row == row_ids, 1.0, 0.0).astype(jnp.bfloat16)
        for c in range(CH):
            for h in range(half):
                pair = [
                    jnp.dot(
                        hot,
                        parts[r * pitch : r * pitch + slots, :].astype(jnp.bfloat16),
                        preferred_element_type=jnp.float32,
                    )
                    for r in (c * HI + h, c * HI + half + h)
                ]
                acc[c * half + h] = jnp.concatenate(pair, axis=1)

        if relaying:

            @pl.when((k == 1) & (outer == 0))
            def _():
                relay_copy().wait_recv()
                acc[...] += dense_got[relay_slot].astype(jnp.float32)

        @pl.when(k < views - 1)
        def _():
            dense_send[k] = acc[...].astype(jnp.bfloat16)
            if relaying:

                @pl.when((k == 0) & (outer == 1))
                def _():
                    relay_copy().start()

                @pl.when((k > 0) | (outer == 0))
                def _():
                    dense_copy(k).start()

            else:
                dense_copy(k).start()

    def add_arrived(k):
        dense_copy(k).wait_recv()
        acc[...] += dense_got[k].astype(jnp.float32)

    if relaying:
        pl.when(outer == 0)(functools.partial(add_arrived, 0))
    else:
        add_arrived(0)

    @pl.loop(1, views - 1)
    def _(k):
        add_arrived(k)

    total = hist[...]
    for k in range(views - 1):
        hist_copy(k).wait_recv()
        total += hist_got[k]
    total_ref[...] = total

    @pl.loop(1, tiles)
    def _(i):
        meta_copy(i).wait_send()

    @pl.loop(0, views)
    def _(k):
        @pl.loop(1, tiles)
        def _(i):
            points_copy(k, i).wait_send()

    @pl.loop(0, views - 1)
    def _(k):
        dense_copy(k).wait_send()
        hist_copy(k).wait_send()


def on_device(tiles, sdf_value, weight, color, voxel_index, valid, list_count, list_key, owner_slot):
    lists, points = sdf_value.shape
    n = lax.axis_size(AXES)
    blocks_all = owner_slot.shape[0]
    blocks_dev = blocks_all // n
    cap = 4 * lists // n
    q = -(-lists // 128)
    views = n // tiles

    meta_rows = -(-(views + 2 * q) // 8) * 8
    payload = (n, (CH + 1) * cap, points)
    wide = (blocks_all // 128, 128)
    rows = CH * HI
    vmem = pl.BlockSpec(memory_space=pltpu.VMEM)
    sums, total = pl.pallas_call(
        functools.partial(join_kernel, views, tiles, cap, q),
        out_shape=(
            jax.ShapeDtypeStruct((rows // 2, blocks_dev, 2 * LO), jnp.float32),
            jax.ShapeDtypeStruct(wide, jnp.float32),
        ),
        in_specs=[vmem] * 8,
        out_specs=(vmem,) * 2,
        scratch_shapes=[
            pltpu.VMEM(payload, jnp.bfloat16),
            pltpu.VMEM((tiles, meta_rows, 128), jnp.float32),
            pltpu.VMEM((CH + 1, lists, points), jnp.bfloat16),
            pltpu.VMEM(payload, jnp.bfloat16),
            pltpu.VMEM((tiles, meta_rows, 128), jnp.float32),
            pltpu.VMEM(((CH + 1) * cap, points), jnp.float32),
            pltpu.VMEM((rows * (tiles * cap + 8), LO), jnp.float32),
            pltpu.VMEM((views - 1, rows // 2, blocks_dev, 2 * LO), jnp.bfloat16),
            pltpu.VMEM((views, rows // 2, blocks_dev, 2 * LO), jnp.bfloat16),
            pltpu.VMEM((blocks_all // 128, 128), jnp.float32),
            pltpu.VMEM((views - 1, blocks_all // 128, 128), jnp.float32),
            pltpu.SemaphoreType.DMA((n,)),
            pltpu.SemaphoreType.DMA((n,)),
            pltpu.SemaphoreType.DMA((tiles,)),
            pltpu.SemaphoreType.DMA((tiles,)),
            pltpu.SemaphoreType.DMA((views - 1,)),
            pltpu.SemaphoreType.DMA((views,)),
            pltpu.SemaphoreType.DMA((views - 1,)),
            pltpu.SemaphoreType.DMA((views - 1,)),
        ],
        compiler_params=pltpu.CompilerParams(collective_id=0, has_side_effects=True),
    )(
        list_key.reshape(1, lists), owner_slot.reshape(wide), list_count.reshape(1, lists),
        sdf_value, weight, color, voxel_index, valid,
    )
    tsdf, joined, counts = pl.pallas_call(
        finish_kernel,
        out_shape=(
            jax.ShapeDtypeStruct((blocks_dev, VOX), jnp.float32),
            jax.ShapeDtypeStruct((3, blocks_dev, VOX), jnp.float32),
            jax.ShapeDtypeStruct(wide, jnp.int32),
        ),
        in_specs=[vmem] * 2,
        out_specs=(vmem,) * 3,
    )(sums, total)
    return tsdf, jnp.swapaxes(joined, 0, 1), counts.reshape(blocks_all)


def solution(mesh):
    return jax.shard_map(
        functools.partial(on_device, mesh.shape["tile"]),
        mesh=mesh,
        in_specs=(
            P(AXES, None),
            P(AXES, None),
            P(None, AXES, None),
            P(AXES, None),
            P(AXES, None),
            P(AXES),
            P(AXES),
            P(),
        ),
        out_specs=(P(AXES, None), P(AXES, None, None), P()),
        check_vma=False,
    )
```
